32 devices in a mesh: src: 16 (over z, y, core), tgt: 2 (over x).
Axes of the slice: x: 2, y: 2, z: 4, core: 2. Of those that a mesh axis runs over, the one named last changes fastest.
Arguments:
- inputs: bfloat16 [64, 2, 1024, 512], P(('src', 'tgt')), may hold values from -6 to 6
- leaf_maps: bfloat16 [64, 2, 256, 1024], P(('src', 'tgt')), may hold values from -0.125 to 0.125
- transfer_blocks: bfloat16 [4, 64, 2, 2, 256, 256], P(None, ('src', 'tgt')), may hold values from -0.1875 to 0.1875
Outputs:
- butterfly_out: bfloat16 [64, 2, 256, 512], P(('src', 'tgt'))
The draws below stay inside these ranges and needn't reach their ends.
All inputs are finite; a program needn't handle non-finite values.
Results may differ from the reference program's by a relative error of at most 0.012.
Values may be sent and summed in bfloat16 or wider, within the bound.
A program may use at most 64 MiB of HBM per device.

```python
import jax
import jax.numpy as jnp
from jax import lax

M = 1024
K = 256
R = 512
LEVELS = 4
LEAVES = 64
N_TGT = 2


def level_of(rng, extent, shards, smallest, high):
    def one(position, shards_of):
        heights = jax.random.uniform(jax.random.fold_in(jax.random.fold_in(rng, 6), position), (shards_of,), jnp.float32, smallest / len(shards), high / len(shards))
        return jnp.repeat(jnp.exp(heights), extent[position] // shards_of).reshape((-1,) + (1,) * (len(extent) - position - 1))

    factor_of = one(*shards[0])
    for cut in shards[1:]:
        factor_of = factor_of * one(*cut)
    return factor_of


def normal_values(rng, shape, deviation, bound, split=(), kind=jnp.bfloat16):
    level = level_of(rng, shape, split, -0.22, 0.18) if split else 1.0
    entries = jax.random.normal(rng, shape, jnp.float32) * deviation * level
    return jnp.minimum(jnp.maximum(entries, -bound), bound).astype(kind)


def setup_inputs(seed: int = 0) -> dict:
    seeds = jax.random.split(jax.random.key(seed), 4)
    return {
        "inputs": normal_values(seeds[0], (LEAVES, 2, M, R), 1.0, 6.0, ((0, 32),)),
        "leaf_maps": normal_values(seeds[1], (LEAVES, 2, K, M), (2 * M) ** -0.5, 0.125, ((0, 32),)),
        "transfer_blocks": normal_values(seeds[2], (LEVELS, LEAVES, 2, 2, K, K), (4 * K) ** -0.5, 0.1875, ((1, 32),)),
    }


def complex_product(blocks, vectors):
    real_part = jnp.dot(blocks[0], vectors[0], preferred_element_type=jnp.float32) - jnp.dot(blocks[1], vectors[1], preferred_element_type=jnp.float32)
    imag_part = jnp.dot(blocks[0], vectors[1], preferred_element_type=jnp.float32) + jnp.dot(blocks[1], vectors[0], preferred_element_type=jnp.float32)
    return jnp.stack([real_part, imag_part])


def butterfly_level(coeffs, blocks, stride):
    groups = LEAVES // (2 * stride)
    paired = coeffs.reshape(groups, 2, stride, 2, K, R).transpose(0, 2, 1, 3, 4, 5).reshape(groups * stride, 2, 2, K, R)
    block_pairs = blocks.reshape(groups, 2, stride, 2, 2, K, K).transpose(0, 2, 1, 3, 4, 5, 6).reshape(groups * stride, 2, 2, 2, K, K)

    def combine_pair(pair_items):
        vectors, pair_blocks = pair_items
        halves = []
        for target_bit in range(2):
            own_term = complex_product(pair_blocks[target_bit, target_bit], vectors[target_bit])
            partner = complex_product(pair_blocks[1 - target_bit, target_bit], vectors[1 - target_bit]).astype(jnp.bfloat16)
            halves.append(own_term + partner.astype(jnp.float32))
        return jnp.stack(halves).astype(jnp.bfloat16)

    updated = lax.map(combine_pair, (paired, block_pairs))
    return updated.reshape(groups, stride, 2, 2, K, R).transpose(0, 2, 1, 3, 4, 5).reshape(LEAVES, 2, K, R)


def reference(inputs, leaf_maps, transfer_blocks):
    coeffs = lax.map(lambda pair_items: complex_product(pair_items[0], pair_items[1]).astype(jnp.bfloat16), (leaf_maps, inputs))
    for level_index, stride in enumerate((1, LEAVES // 2, LEAVES // 4, N_TGT)):
        coeffs = butterfly_level(coeffs, transfer_blocks[level_index], stride)
    return coeffs
```

```python
import functools

import jax
import jax.numpy as jnp
from jax import lax
from jax.experimental import pallas as pl
from jax.experimental.pallas import tpu as pltpu
from jax.sharding import PartitionSpec as P

MESH = pl.DeviceIdType.MESH
LANES = 128


def product(blocks, vectors):
    rows = blocks.shape[0] // 2
    width = vectors.shape[1] // 2
    both = jnp.dot(blocks, vectors, preferred_element_type=jnp.float32)
    real_part = both[:rows, :width] - both[rows:, width:]
    imag_part = both[:rows, width:] + both[rows:, :width]
    return jnp.concatenate([real_part, imag_part], axis=1)


def kernel(
    sizes,
    inputs,
    leaf_maps,
    transfer,
    out,
    x_in,
    maps,
    blocks,
    coeffs,
    send1,
    relay_a,
    relay_b,
    recv1,
    send2,
    recv2,
    send3,
    recv3,
    result,
    in_sem,
    maps_sem,
    blocks_sem,
    out_sem,
    s1_sem,
    ra_sem,
    rb_sem,
    fa_sem,
    fb_sem,
    r1_sem,
    s2_sem,
    r2_sem,
    s3_sem,
    r3_sem,
):
    src_bits, tgt_bits, levels, chunks = sizes
    units = 2 * chunks
    src, tgt = lax.axis_index("src"), lax.axis_index("tgt")
    hi, lo = 2 ** (src_bits - 1), 2 ** (src_bits - 2)
    far = 2 ** (tgt_bits - 1)
    bit1, bit2, bit3 = src // hi % 2, src // lo % 2, tgt // far % 2
    flip_lo = src + lo - 2 * lo * bit2
    flip_both = flip_lo + hi - 2 * hi * bit1
    near = (flip_lo, tgt)
    across = (flip_both, tgt)
    side = (src, tgt + far - 2 * far * bit3)
    is_end = bit1 == bit2
    is_mid = bit1 != bit2

    barrier = pltpu.get_barrier_semaphore()
    for peer in (near, across, side):
        pl.semaphore_signal(barrier, inc=1, device_id=peer, device_id_type=MESH)

    def load_in(c, n, part):
        return pltpu.make_async_copy(
            inputs.at[n, part, :, pl.ds(pl.multiple_of(c * LANES, LANES), LANES)],
            x_in.at[c, n, :, pl.ds(part * LANES, LANES)],
            in_sem.at[c, n, part],
        )

    def load_maps(n):
        return pltpu.make_async_copy(leaf_maps.at[n], maps.at[n], maps_sem.at[n])

    def load_blocks(v):
        return pltpu.make_async_copy(transfer.at[v], blocks.at[v], blocks_sem.at[v])

    for n in range(2):
        load_maps(n).start()
        for part in range(2):
            load_in(0, n, part).start()
    load_blocks(0).start()
    load_blocks(1).start()
    for c in range(1, chunks):
        for n in range(2):
            for part in range(2):
                load_in(c, n, part).start()
    for v in range(2, levels):
        load_blocks(v).start()

    def remote(source, target, send_sem, recv_sem, peer):
        return pltpu.make_async_remote_copy(
            src_ref=source,
            dst_ref=target,
            send_sem=send_sem,
            recv_sem=recv_sem,
            device_id=peer,
            device_id_type=MESH,
        )

    def own_a(u):
        return remote(send1.at[u], relay_a.at[u], s1_sem.at[u], ra_sem.at[u], near)

    def own_b(u):
        return remote(send1.at[u], relay_b.at[u], s1_sem.at[u], rb_sem.at[u], across)

    def forward_a(u):
        return remote(relay_a.at[u], recv1.at[u], fa_sem.at[u], r1_sem.at[u], across)

    def forward_b(u):
        return remote(relay_b.at[u], recv1.at[u], fb_sem.at[u], r1_sem.at[u], near)

    def second(u):
        return remote(send2.at[u], recv2.at[u], s2_sem.at[u], r2_sem.at[u], near)

    def third(u):
        return remote(send3.at[u], recv3.at[u], s3_sem.at[u], r3_sem.at[u], side)

    def forward(u):
        own_b(u).wait_recv()
        forward_b(u).start()
        own_a(u).wait_recv()
        forward_a(u).start()

    def store(u, part):
        return pltpu.make_async_copy(
            result.at[u, :, pl.ds(part * LANES, LANES)],
            out.at[u % 2, part, :, pl.ds(pl.multiple_of(u // 2 * LANES, LANES), LANES)],
            out_sem.at[u, part],
        )

    def pre(c):
        vectors = []
        for n in range(2):
            for part in range(2):
                load_in(c, n, part).wait()
            vectors.append(product(maps[n], x_in[c, n]).astype(jnp.bfloat16))

        @pl.when(c == 0)
        def _():
            load_blocks(0).wait()
            load_blocks(1).wait()

        for n in range(2):
            own_term = product(blocks[0, n, n], vectors[n])
            partner = product(blocks[0, 1 - n, n], vectors[1 - n]).astype(jnp.bfloat16)
            updated = (own_term + partner.astype(jnp.float32)).astype(jnp.bfloat16)
            u = 2 * c + n
            coeffs[u] = updated
            send1[u] = product(blocks[1, n, 1 - bit1], updated).astype(jnp.bfloat16)
            if n == 0:

                @pl.when(c == 0)
                def _():
                    pl.semaphore_wait(barrier, 3)

            @pl.when(is_end)
            def _():
                own_a(u).start()

            @pl.when(is_mid)
            def _():
                own_b(u).start()

    def level(v, u, bit, arrived):
        local_term = product(blocks[v, u % 2, bit], coeffs[u])
        return (local_term + arrived[u].astype(jnp.float32)).astype(jnp.bfloat16)

    def post1(u):
        forward_a(u).wait_recv()
        updated = level(1, u, bit1, recv1)
        coeffs[u] = updated
        send2[u] = product(blocks[2, u % 2, 1 - bit2], updated).astype(jnp.bfloat16)
        second(u).start()

    def post2(u):
        second(u).wait_recv()
        updated = level(2, u, bit2, recv2)
        coeffs[u] = updated
        send3[u] = product(blocks[3, u % 2, 1 - bit3], updated).astype(jnp.bfloat16)
        third(u).start()

    def post3(u):
        third(u).wait_recv()
        result[u] = level(3, u, bit3, recv3)
        for part in range(2):
            store(u, part).start()

    for n in range(2):
        load_maps(n).wait()

    @pl.loop(0, chunks)
    def _(c):
        pre(c)

        @pl.when(jnp.logical_and(is_mid, c > 0))
        def _():
            forward(c - 1)

    for v in range(2, levels):
        load_blocks(v).wait()

    @pl.when(is_mid)
    def _():
        @pl.loop(chunks - 1, units)
        def _(u):
            forward(u)

    @pl.when(is_end)
    def _():
        @pl.loop(0, units)
        def _(u):
            post1(u)

    @pl.loop(0, units + 2)
    def _(u):
        @pl.when(jnp.logical_and(is_mid, u < units))
        def _():
            post1(u)

        @pl.when(jnp.logical_and(u >= 1, u < units + 1))
        def _():
            post2(u - 1)

        @pl.when(u >= 2)
        def _():
            post3(u - 2)

    @pl.loop(0, units)
    def _(u):
        own_a(u).wait_send()
        second(u).wait_send()
        third(u).wait_send()
        for part in range(2):
            store(u, part).wait()

        @pl.when(is_mid)
        def _():
            forward_a(u).wait_send()
            forward_b(u).wait_send()


def local(inputs, leaf_maps, transfer_blocks):
    nodes, _, depth, columns = inputs.shape
    rank = leaf_maps.shape[2]
    levels = transfer_blocks.shape[0]
    chunks = columns // LANES
    units = nodes * chunks
    src_bits = lax.axis_size("src").bit_length() - 1
    tgt_bits = lax.axis_size("tgt").bit_length() - 1
    maps = leaf_maps.reshape(nodes, 2 * rank, depth)
    blocks = transfer_blocks.reshape(levels, nodes, 2, 2 * rank, rank)
    unit = pltpu.VMEM((units, rank, 2 * LANES), jnp.bfloat16)
    dma = pltpu.SemaphoreType.DMA
    return pl.pallas_call(
        functools.partial(kernel, (src_bits, tgt_bits, levels, chunks)),
        out_shape=jax.ShapeDtypeStruct((nodes, 2, rank, columns), jnp.bfloat16),
        in_specs=[pl.BlockSpec(memory_space=pl.ANY)] * 3,
        out_specs=pl.BlockSpec(memory_space=pl.ANY),
        scratch_shapes=[
            pltpu.VMEM((chunks, nodes, depth, 2 * LANES), jnp.bfloat16),
            pltpu.VMEM(maps.shape, jnp.bfloat16),
            pltpu.VMEM(blocks.shape, jnp.bfloat16),
        ]
        + [unit] * 10
        + [
            dma((chunks, nodes, 2)),
            dma((nodes,)),
            dma((levels,)),
            dma((units, 2)),
        ]
        + [dma((units,))] * 10,
        compiler_params=pltpu.CompilerParams(
            collective_id=0, has_side_effects=True, vmem_limit_bytes=60 * 2**20
        ),
    )(inputs, maps, blocks)


def solution(mesh):
    placed = (
        P(("src", "tgt"), None, None, None),
        P(("src", "tgt"), None, None, None),
        P(None, ("src", "tgt"), None, None, None, None),
    )
    return jax.shard_map(
        local,
        mesh=mesh,
        in_specs=placed,
        out_specs=P(("src", "tgt"), None, None, None),
        check_vma=False,
    )
```
